32 devices in a mesh: dp: 2 (over x), row: 4 (over y, core), col: 4 (over z).
Axes of the slice: x: 2, y: 2, z: 4, core: 2. Of those that a mesh axis runs over, the one named last changes fastest.
Arguments:
- tokens: bfloat16 [768, 4096], P('row', ('dp', 'col')), may hold values from -40 to 40
- segments: int32 [8, 512], P(('dp', 'row')), may hold values from 0 to 2, never falling along the last dimension, each value on 1 to 256 neighbouring positions
- gain_one: float32 [768], P('row'), may hold values from 0.1 to 1.9
- qkv_weight: bfloat16 [768, 2304], P('row', 'col'), may hold values from -0.21875 to 0.21875
- out_weight: bfloat16 [768, 768], P('col', 'row'), may hold values from -0.625 to 0.625
- gain_two: float32 [768], P('row'), may hold values from 0.1 to 1.9
- in_weight: bfloat16 [768, 2, 1152], P('row', None, 'col'), may hold values from -0.21875 to 0.21875
- down_weight: bfloat16 [1152, 768], P('col', 'row'), may hold values from -0.1875 to 0.1875
- grad_output: bfloat16 [768, 4096], P('row', ('dp', 'col')), may hold values from -6 to 6
Outputs:
- output: float32 [768, 4096], P('row', ('dp', 'col'))
- grad_tokens: float32 [768, 4096], P('row', ('dp', 'col'))
- grad_gain_one: float32 [768], P('row')
- grad_qkv: float32 [768, 2304], P('row', 'col')
- grad_out: float32 [768, 768], P('col', 'row')
- grad_gain_two: float32 [768], P('row')
- grad_in: float32 [768, 2, 1152], P('row', None, 'col')
- grad_down: float32 [1152, 768], P('col', 'row')
The draws below stay inside these ranges and needn't reach their ends.
Inputs may be any that keep to these rules, and one draw needn't show every extreme that they name: `segments`: within each packed sequence the numbers never fall, each of the 3 numbers covers 1 to 256 positions, and one covers exactly 256.
All inputs are finite; a program needn't handle non-finite values.
Results may differ from the reference program's by a relative error of at most 0.015.
Values may be sent and summed in bfloat16 or wider, within the bound.
No kernel may reach another device: no remote copies, remote signals or barrier semaphores. Data moves between devices by JAX's collectives and lax.ppermute only.
A program may use at most 64 MiB of HBM per device.

```python
import math
import jax
import jax.numpy as jnp
import numpy as np
from jax import lax

D = 768
HEADS = 12
FF = 1152
HD = 64
SEQ = 512
WINDOW = 128
NSEG = 3
TOKENS = 4096
SEQS = 8


def draw_tokens(key, part):
    key_noise, key_rows, key_cols, key_shift = jax.random.split(key, 4)
    row_scale = jnp.exp(jax.random.uniform(key_rows, (TOKENS, 1), jnp.float32, math.log(0.3), math.log(3.0)))
    col_scale = jnp.exp(jax.random.uniform(key_cols, (1, D), jnp.float32, math.log(0.3), math.log(3.0)))
    row_shift = jnp.clip(0.5 * jax.random.normal(key_shift, (TOKENS, 1), jnp.float32), -1.0, 1.0)
    noise_field = jnp.clip(jax.random.normal(key_noise, (TOKENS, D), jnp.float32), -4.0, 4.0)
    return (row_scale * (col_scale * noise_field + row_shift)).T.astype(jnp.bfloat16)


def level_of(key, extent, pieces, smallest, top_value):
    level = 1.0
    for axis_at, parts in pieces:
        heights = jax.random.uniform(jax.random.fold_in(jax.random.fold_in(key, 6), axis_at), (parts,), jnp.float32, smallest / len(pieces), top_value / len(pieces))
        level = level * jnp.repeat(jnp.exp(heights), extent[axis_at] // parts).reshape((-1,) + (1,) * (len(extent) - 1 - axis_at))
    return level


def profile(number_of, total, reach, skew):
    portions = [(1 << 20) // math.isqrt(grade ** skew) + 1 for grade in range(2, number_of + 1)]
    spare, counts = total - reach - (number_of - 1), [1] * (number_of - 1)
    while spare > 0:
        movable = [i for i in range(number_of - 1) if counts[i] < reach]
        whole, budget = sum([portions[i] for i in movable]), spare
        for i in movable:
            more = min(reach - counts[i], max(1, budget * portions[i] // whole), spare)
            counts[i] = counts[i] + more
            spare = spare - more
    return np.array([reach] + counts)


def ragged_sizes(own_key, count, total, bound, slope):
    if count == 2:
        one = jax.random.randint(own_key, (), max(1, total - bound), min(bound, total - 1) + 1)
        return jnp.stack([one, total - one])
    lengths = jnp.asarray(profile(count, total, bound, slope), jnp.int32)
    couples = (count - 1) // 2
    source_of, receiver = lengths[1:1 + 2 * couples:2], lengths[2:2 + 2 * couples:2]
    room = jnp.minimum(source_of - 1, bound - receiver)
    passed = jax.random.randint(jax.random.fold_in(own_key, 1), (couples,), 0, 1 << 20) % (room + 1)
    lengths = lengths.at[1:1 + 2 * couples:2].set(source_of - passed).at[2:2 + 2 * couples:2].set(receiver + passed)
    return lengths[jax.random.permutation(jax.random.fold_in(own_key, 2), count)]


def noise(stream_key, shape, scale, limit, shards=(), held_as=jnp.bfloat16):
    values = jax.random.normal(stream_key, shape, jnp.float32) * scale
    if len(shards) > 0:
        values = level_of(stream_key, shape, shards, -0.22, 0.18) * values
    return jnp.clip(values, min=-limit, max=limit).astype(held_as)


def setup_inputs(seed: int = 0) -> dict:
    key_list = jax.random.split(jax.random.key(seed), 10)
    tokens = draw_tokens(jax.random.fold_in(key_list[9], 71), 0)
    segments = jax.vmap(lambda own: jnp.searchsorted(jnp.cumsum(ragged_sizes(own, NSEG, SEQ, SEQ // 2, 0)), jnp.arange(SEQ), side="right"))(jax.random.split(key_list[1], SEQS)).reshape((SEQS, SEQ)).astype(jnp.int32)
    gain_one = jnp.clip(1.0 + 0.18 * jax.random.normal(key_list[2], (D,), jnp.float32), 0.1, 1.9)
    qkv_weight = noise(key_list[3], (D, 3 * D), D ** -0.5, 0.21875, ((0, 4), (1, 4)))
    out_weight = noise(key_list[4], (D, D), (D // 8) ** -0.5, 0.625, ((0, 4), (1, 4)))
    gain_two = jnp.clip(1.0 + 0.18 * jax.random.normal(key_list[5], (D,), jnp.float32), 0.1, 1.9)
    in_weight = noise(key_list[6], (D, 2, FF), D ** -0.5, 0.21875, ((0, 4), (2, 4)))
    down_weight = noise(key_list[7], (FF, D), FF ** -0.5, 0.1875, ((0, 4), (1, 4)))
    grad_output = noise(key_list[8], (D, TOKENS), 1.0, 6.0, ((0, 4), (1, 8)))
    return dict(tokens=tokens, segments=segments, gain_one=gain_one, qkv_weight=qkv_weight, out_weight=out_weight, gain_two=gain_two, in_weight=in_weight, down_weight=down_weight, grad_output=grad_output)


EPS = 1e-05
THETA = 10000.0

def product(left, right):
    return jnp.dot(left.astype(jnp.float32), right.astype(jnp.float32), precision=lax.Precision.HIGHEST)

def rope_tables(length, head_size):
    places = jnp.arange(length).astype(jnp.float32)
    inverse = THETA ** (-jnp.arange(0, head_size, 2).astype(jnp.float32) / head_size)
    angles = places[:, None] * inverse[None, :]
    cos_table = jnp.concatenate([jnp.cos(angles), jnp.cos(angles)], 1)
    sine_table = jnp.concatenate([jnp.sin(angles), jnp.sin(angles)], 1)
    return (cos_table[:, None, :], sine_table[:, None, :])

def rotate(field, cos_table, sine_table):
    half_size = field.shape[-1] // 2
    turned = jnp.concatenate([-field[..., half_size:], field[..., :half_size]], -1)
    return field * cos_table + turned * sine_table

def rotate_back(grad_field, cos_table, sine_table):
    half_size = grad_field.shape[-1] // 2
    scaled = grad_field * sine_table
    turned = jnp.concatenate([scaled[..., half_size:], -scaled[..., :half_size]], -1)
    return grad_field * cos_table + turned

def allowed_pairs(segment_row):
    places = jnp.arange(segment_row.shape[0])
    same_doc = segment_row[:, None] == segment_row[None, :]
    nearby = jnp.abs(places[:, None] - places[None, :]) <= WINDOW // 2
    return same_doc & nearby

def gelu_parts(field):
    normal_cdf = 0.5 * (1.0 + lax.erf(field * 0.7071067811865476))
    normal_pdf = jnp.exp(-0.5 * field * field) * 0.3989422804014327
    return (field * normal_cdf, normal_cdf + field * normal_pdf)

def layer_norm(field):
    mean_val = lax.optimization_barrier(jnp.mean(field, -1, keepdims=True))
    square = lax.optimization_barrier(jnp.mean(field * field, -1, keepdims=True))
    inv_std = lax.rsqrt(square - mean_val * mean_val + EPS)
    return ((field - mean_val) * inv_std, inv_std)

def norm_backward(grad_norm, normed, inv_std, gain):
    scaled = grad_norm * gain
    first = lax.optimization_barrier(jnp.mean(scaled, -1, keepdims=True))
    second = lax.optimization_barrier(jnp.mean(scaled * normed, -1, keepdims=True))
    return inv_std * (scaled - first - normed * second)

def attend_forward(qkv_rows, segment_row):
    length = qkv_rows.shape[0]
    shaped = qkv_rows.reshape(length, HEADS, 3, HD)
    cos_table, sine_table = rope_tables(length, HD)
    queries = rotate(shaped[:, :, 0], cos_table, sine_table).astype(jnp.bfloat16)
    keys_rot = rotate(shaped[:, :, 1], cos_table, sine_table).astype(jnp.bfloat16)
    values = shaped[:, :, 2].astype(jnp.bfloat16)
    allowed = allowed_pairs(segment_row)
    scores = jnp.einsum('shd,thd->hst', queries.astype(jnp.float32), keys_rot.astype(jnp.float32), precision=lax.Precision.HIGHEST) * HD ** (-0.5)
    exp_scores = jnp.where(allowed[None], jnp.exp(scores), 0.0)
    totals = lax.optimization_barrier(jnp.sum(exp_scores, -1))
    attn_probs = (exp_scores / totals[..., None]).astype(jnp.bfloat16)
    attended = jnp.einsum('hst,thd->shd', attn_probs.astype(jnp.float32), values.astype(jnp.float32), precision=lax.Precision.HIGHEST)
    return (attended, jnp.log(totals), queries, keys_rot, values)

def attend_backward(queries, keys_rot, values, log_totals, attended, grad_att, segment_row):
    length = queries.shape[0]
    cos_table, sine_table = rope_tables(length, HD)
    allowed = allowed_pairs(segment_row)
    query_f = queries.astype(jnp.float32)
    key_f = keys_rot.astype(jnp.float32)
    highest = lax.Precision.HIGHEST
    scores = jnp.einsum('shd,thd->hst', query_f, key_f, precision=highest) * HD ** (-0.5)
    probs_back = jnp.where(allowed[None], jnp.exp(scores - log_totals[..., None]), 0.0)
    grad_round = grad_att.astype(jnp.bfloat16).astype(jnp.float32)
    deltas = lax.optimization_barrier(jnp.sum(grad_att * attended, -1))
    grad_probs = jnp.einsum('shd,thd->hst', grad_round, values.astype(jnp.float32), precision=highest)
    probs_round = probs_back.astype(jnp.bfloat16).astype(jnp.float32)
    grad_values = jnp.einsum('hst,shd->thd', probs_round, grad_round, precision=highest)
    grad_scores = (probs_back * (grad_probs - deltas.T[:, :, None])).astype(jnp.bfloat16).astype(jnp.float32)
    grad_queries = jnp.einsum('hst,thd->shd', grad_scores, key_f, precision=highest) * HD ** (-0.5)
    grad_keys = jnp.einsum('hst,shd->thd', grad_scores, query_f, precision=highest) * HD ** (-0.5)
    stacked = jnp.stack([rotate_back(grad_queries, cos_table, sine_table), rotate_back(grad_keys, cos_table, sine_table), grad_values], 2)
    return stacked.reshape(length, 3 * HEADS * HD).astype(jnp.bfloat16)

def reference(tokens, segments, gain_one, qkv_weight, out_weight, gain_two, in_weight, down_weight, grad_output):
    model_width = tokens.shape[0]
    row_count = tokens.shape[1]
    inputs = tokens.T.astype(jnp.float32)
    grad_rows = grad_output.T
    norm_one, inv_one = layer_norm(inputs)
    h_one = (norm_one * gain_one).astype(jnp.bfloat16)
    qkv_rows = product(h_one, qkv_weight)

    def forward_seq(pair):
        return attend_forward(pair[0], pair[1])
    attended, log_totals, queries, keys_rot, values = lax.map(forward_seq, (qkv_rows.reshape(SEQS, SEQ, 3 * model_width), segments))
    attended_b = attended.reshape(row_count, model_width).astype(jnp.bfloat16)
    residual = inputs + product(attended_b, out_weight)
    norm_two, inv_two = layer_norm(residual)
    h_two = (norm_two * gain_two).astype(jnp.bfloat16)
    feed_pre = product(h_two, in_weight.reshape(model_width, 2 * FF)).reshape(row_count, 2, FF)
    gelu_val, gelu_slope = gelu_parts(feed_pre[:, 0])
    hidden = (gelu_val * feed_pre[:, 1]).astype(jnp.bfloat16)
    output = residual + product(hidden, down_weight)
    grad_hidden = product(grad_rows, down_weight.T)
    grad_down = product(hidden.T, grad_rows)
    grad_feed = jnp.stack([grad_hidden * feed_pre[:, 1] * gelu_slope, grad_hidden * gelu_val], 1).astype(jnp.bfloat16)
    grad_flat = grad_feed.reshape(row_count, 2 * FF)
    grad_two = product(grad_flat, in_weight.reshape(model_width, 2 * FF).T)
    grad_in = product(h_two.T, grad_flat).reshape(model_width, 2, FF)
    grad_gain_two = lax.optimization_barrier(jnp.sum(grad_two * norm_two, 0))
    grad_resid = grad_rows.astype(jnp.float32) + norm_backward(grad_two, norm_two, inv_two, gain_two)
    grad_resid_b = grad_resid.astype(jnp.bfloat16)
    grad_att = product(grad_resid_b, out_weight.T)
    grad_out = product(attended_b.T, grad_resid_b)

    def backward_seq(items):
        return attend_backward(items[0], items[1], items[2], items[3], items[4], items[5], items[6])
    grad_qkvrows = lax.map(backward_seq, (queries, keys_rot, values, log_totals, attended, grad_att.reshape(SEQS, SEQ, HEADS, HD), segments))
    grad_qkvrows = grad_qkvrows.reshape(row_count, 3 * model_width)
    grad_one = product(grad_qkvrows, qkv_weight.T)
    grad_qkv = product(h_one.T, grad_qkvrows)
    grad_gain_one = lax.optimization_barrier(jnp.sum(grad_one * norm_one, 0))
    grad_tokens = grad_resid + norm_backward(grad_one, norm_one, inv_one, gain_one)
    return (output.T, grad_tokens.T, grad_gain_one, grad_qkv, grad_out, grad_gain_two, grad_in, grad_down)
```

```python
import jax
import jax.numpy as jnp
from jax import lax
from jax.experimental import pallas as pl
from jax.experimental.pallas import tpu as pltpu
from jax.sharding import PartitionSpec as P

HD = 64
WINDOW = 128
EPS = 1e-05
THETA = 10000.0


bf16 = jnp.bfloat16
f32 = jnp.float32


def dot(left, right, left_dim, right_dim):
    return lax.dot_general(
        left, right, (((left_dim,), (right_dim,)), ((), ())), preferred_element_type=f32
    )


def layer_norm(field):
    mean_val = jnp.mean(field, -1, keepdims=True)
    square = jnp.mean(field * field, -1, keepdims=True)
    inv_std = lax.rsqrt(square - mean_val * mean_val + EPS)
    return ((field - mean_val) * inv_std, inv_std)


def norm_backward(grad_norm, normed, inv_std, gain):
    scaled = grad_norm * gain
    first = jnp.mean(scaled, -1, keepdims=True)
    second = jnp.mean(scaled * normed, -1, keepdims=True)
    return inv_std * (scaled - first - normed * second)


def lane_in_head(shape):
    return lax.broadcasted_iota(jnp.int32, shape, 1) % HD


def attend_kernel(
    h_ref, x_ref, near_ref, far_ref, cos_ref, sine_ref, mask_ref,
    qkv_ref, probs_ref, att_ref, res_ref,
):
    half = near_ref.shape[1]
    tokens = x_ref.shape[0]
    heads = probs_ref.shape[1]
    edge = WINDOW // 2
    width = qkv_ref.shape[2]
    used = heads * 3 * HD

    @pl.when(pl.program_id(0) == 0)
    def _():
        res_ref[...] = x_ref[...]

    rows = dot(h_ref[:, :half], near_ref[0, :, :width], 1, 0) + dot(
        h_ref[:, half:], far_ref[0, :, :width], 1, 0
    )
    low = lane_in_head(rows.shape) < HD // 2
    turned = jnp.where(
        low, -pltpu.roll(rows, width - HD // 2, 1), pltpu.roll(rows, HD // 2, 1)
    )
    qkv_ref[0] = (rows * cos_ref[...] + turned * sine_ref[...]).astype(bf16)
    allowed = mask_ref[...] > 0.0
    for head in range(heads):
        at = head * 3 * HD
        query = qkv_ref[0, edge : edge + tokens, at : at + HD]
        key = qkv_ref[0, :, at + HD : at + 2 * HD]
        value = qkv_ref[0, :, at + 2 * HD : at + 3 * HD]
        scores = dot(query, key, 1, 1) * HD ** (-0.5)
        exps = jnp.where(allowed, jnp.exp(scores), 0.0)
        probs = exps / jnp.sum(exps, -1, keepdims=True)
        probs_ref[0, head] = probs
        att_ref[0, :, head * HD : (head + 1) * HD] = dot(probs.astype(bf16), value, 1, 0)
    att = att_ref[0].astype(bf16)
    res_ref[:, :half] += dot(att, near_ref[0, :, used:], 1, 1)
    res_ref[:, half:] += dot(att, far_ref[0, :, used:], 1, 1)


def feed_kernel(
    h_ref, gy_ref, res_ref, near_ref, far_ref,
    out_ref, two_ref, own_ref, sib_ref, feed_ref,
):
    half = near_ref.shape[1]
    part = near_ref.shape[2] // 3

    @pl.when(pl.program_id(0) == 0)
    def _():
        out_ref[...] = res_ref[...]
        two_ref[...] = jnp.zeros_like(two_ref)

    pre = dot(h_ref[:, :half], near_ref[0, :, : 2 * part], 1, 0) + dot(
        h_ref[:, half:], far_ref[0, :, : 2 * part], 1, 0
    )
    gate = pre[:, :part]
    linear = pre[:, part:]
    cdf = 0.5 * (1.0 + lax.erf(gate * 0.7071067811865476))
    pdf = jnp.exp(-0.5 * gate * gate) * 0.3989422804014327
    gelu = gate * cdf
    hidden = (gelu * linear).astype(bf16)
    out_ref[:, :half] += dot(hidden, near_ref[0, :, 2 * part :], 1, 1)
    out_ref[:, half:] += dot(hidden, far_ref[0, :, 2 * part :], 1, 1)
    grad_hidden = dot(gy_ref[:, :half], near_ref[0, :, 2 * part :], 1, 0) + dot(
        gy_ref[:, half:], far_ref[0, :, 2 * part :], 1, 0
    )
    feed_ref[:, :part] = (grad_hidden * linear * (cdf + gate * pdf)).astype(bf16)
    feed_ref[:, part:] = (grad_hidden * gelu).astype(bf16)
    grad_feed = feed_ref[...]
    two_ref[:, :half] += dot(grad_feed, near_ref[0, :, : 2 * part], 1, 1)
    two_ref[:, half:] += dot(grad_feed, far_ref[0, :, : 2 * part], 1, 1)
    own_ref[0, :, : 2 * part] = dot(h_ref[:, :half], grad_feed, 0, 0).astype(bf16)
    own_ref[0, :, 2 * part :] = dot(gy_ref[:, :half], hidden, 0, 0).astype(bf16)
    sib_ref[0, :, : 2 * part] = dot(h_ref[:, half:], grad_feed, 0, 0).astype(bf16)
    sib_ref[0, :, 2 * part :] = dot(gy_ref[:, half:], hidden, 0, 0).astype(bf16)


def attend_back_kernel(
    grad_ref, h_ref, near_ref, far_ref, qkv_ref, probs_ref, att_ref, cos_ref, sine_ref,
    one_ref, own_ref, sib_ref, rows_ref,
):
    half = near_ref.shape[1]
    tokens = grad_ref.shape[0]
    heads = probs_ref.shape[1]
    edge = WINDOW // 2
    width = qkv_ref.shape[2]
    used = heads * 3 * HD
    scale = HD ** (-0.5)

    @pl.when(pl.program_id(0) == 0)
    def _():
        one_ref[...] = jnp.zeros_like(one_ref)
        rows_ref[...] = jnp.zeros_like(rows_ref)

    grad_att = dot(grad_ref[:, :half], near_ref[0, :, used:], 1, 0) + dot(
        grad_ref[:, half:], far_ref[0, :, used:], 1, 0
    )
    for head in range(heads):
        at = head * 3 * HD
        query = qkv_ref[0, edge : edge + tokens, at : at + HD]
        key = qkv_ref[0, :, at + HD : at + 2 * HD]
        value = qkv_ref[0, :, at + 2 * HD : at + 3 * HD]
        grad = grad_att[:, head * HD : (head + 1) * HD]
        rounded = grad.astype(bf16)
        delta = jnp.sum(grad * att_ref[0, :, head * HD : (head + 1) * HD], -1, keepdims=True)
        probs = probs_ref[0, head]
        grad_probs = dot(rounded, value, 1, 1)
        grad_scores = (probs * (grad_probs - delta)).astype(bf16)
        rows_ref[edge : edge + tokens, at : at + HD] = dot(grad_scores, key, 1, 0) * scale
        rows_ref[:, at + HD : at + 2 * HD] = dot(grad_scores, query, 0, 0) * scale
        rows_ref[:, at + 2 * HD : at + 3 * HD] = dot(probs.astype(bf16), rounded, 0, 0)
    rows = rows_ref[...]
    scaled = rows * sine_ref[...]
    low = lane_in_head(rows.shape) < HD // 2
    turned = jnp.where(
        low, pltpu.roll(scaled, width - HD // 2, 1), -pltpu.roll(scaled, HD // 2, 1)
    )
    grad_rows = (rows * cos_ref[...] + turned).astype(bf16)[:, :used]
    att = att_ref[0].astype(bf16)
    one_ref[:, :half] += dot(grad_rows, near_ref[0, :, :used], 1, 1)
    one_ref[:, half:] += dot(grad_rows, far_ref[0, :, :used], 1, 1)
    own_ref[0, :, :used] = dot(h_ref[:, :half], grad_rows, 0, 0).astype(bf16)
    own_ref[0, :, used:] = dot(grad_ref[:, :half], att, 0, 0).astype(bf16)
    sib_ref[0, :, :used] = dot(h_ref[:, half:], grad_rows, 0, 0).astype(bf16)
    sib_ref[0, :, used:] = dot(grad_ref[:, half:], att, 0, 0).astype(bf16)


def whole(shape):
    return pl.BlockSpec(shape, lambda k: (0,) * len(shape))


def slot(shape):
    return pl.BlockSpec((1,) + shape, lambda k: (k,) + (0,) * len(shape))


def shape_of(shape, dtype):
    return jax.ShapeDtypeStruct(shape, dtype)


def make_body(mesh):
    n_dp, n_row, n_col = (mesh.shape[name] for name in ("dp", "row", "col"))

    def by_row(value, flip):
        return lax.ppermute(value, "row", [(i, i ^ flip) for i in range(n_row)])

    def core_swap(value):
        return by_row(value, 1)

    def y_swap(value):
        return by_row(value, 2)

    def x_swap(value):
        return lax.ppermute(value, "dp", [(i, i ^ 1) for i in range(n_dp)])

    def col_shift(value, step):
        return lax.ppermute(value, "col", [(i, (i + step) % n_col) for i in range(n_col)])

    flips = (0, 2, 1, 3)

    def gather_group(shard):
        own = shard[0]
        near = jnp.concatenate([shard, y_swap(shard)], 0)
        others = jnp.stack([col_shift(own, k) for k in range(1, n_col)])
        over_y = y_swap(others)
        over_x = x_swap(others)
        corner = x_swap(over_y)
        rest = jnp.stack([others, over_x, over_y, corner], 1)
        near = near.reshape(1, -1, shard.shape[-1])
        rest = rest.reshape(n_col - 1, -1, shard.shape[-1])
        ours = jnp.concatenate([near, rest], 0)
        theirs = jnp.concatenate([core_swap(near), core_swap(rest)], 0)
        return ours, theirs

    def add(first, *others):
        total = first.astype(f32)
        for other in others:
            total = total + other.astype(f32)
        return total.astype(bf16)

    def reduce_group(own, sib):
        slots, rows, width = own.shape
        quarter = rows // 4
        total = add(own, core_swap(sib)).reshape(slots, 2, 2, quarter, width)
        half = slots // 2
        first, second = total[:half], total[half:]
        over_y = y_swap(first[:, 1])
        over_x = x_swap(second[:, :, 1])
        first = add(first[:, 0], over_y)
        second = add(second[:, :, 0], over_x)
        first = add(first[:, 0], x_swap(first[:, 1]))
        second = add(second[:, 0], y_swap(second[:, 1]))
        pieces = jnp.concatenate([first, second], 0)
        done = add(pieces[0], *[col_shift(pieces[k], -k) for k in range(1, slots)])
        if n_dp > 2:
            groups = [list(range(s, n_dp, 2)) for s in range(2)]
            done = lax.psum(done.astype(f32), "dp", axis_index_groups=groups).astype(bf16)
        return done, x_swap(done)

    def body(
        tokens, segments, gain_one, qkv_weight, out_weight, gain_two, in_weight,
        down_weight, grad_output,
    ):
        features, seq = tokens.shape
        own_len = seq // n_row
        edge = WINDOW // 2
        span = own_len + 2 * edge
        width_all = features * n_row
        fb = features // 2
        row = lax.axis_index("row")
        side = lax.axis_index("dp") % 2

        def turn(value):
            return jnp.where(side == 0, value, jnp.roll(value, fb, 0))

        qkv_cols = qkv_weight.shape[1]
        feed_cols = 2 * in_weight.shape[2]
        att_group = turn(jnp.concatenate([qkv_weight, out_weight.T], 1))
        feed_group = turn(
            jnp.concatenate([in_weight.reshape(features, feed_cols), down_weight.T], 1)
        )
        att_near, att_far = gather_group(att_group.reshape(2, fb, -1))

        turned_tokens = turn(tokens)
        turned_grads = turn(grad_output)
        padded = jnp.pad(turned_tokens, ((0, 0), (edge, edge)))
        payloads = jnp.stack(
            [
                jnp.concatenate(
                    [
                        padded[:, p * own_len : p * own_len + span],
                        turned_grads[:, p * own_len : (p + 1) * own_len],
                    ],
                    1,
                )
                for p in range(n_row)
            ]
        )
        gains = turn(jnp.stack([gain_one, gain_two], 1))
        fields, gain_parts = [], []
        for flip in flips:
            mine = lax.dynamic_index_in_dim(payloads, row ^ flip, 0, keepdims=False)
            fields.append(mine if flip == 0 else by_row(mine, flip))
            gain_parts.append(gains if flip == 0 else by_row(gains, flip))
        field = jnp.concatenate(fields, 0).T
        gain_all = jnp.concatenate(gain_parts, 0).T
        gain_a, gain_b = gain_all[0:1], gain_all[1:2]
        inputs = field[:span].astype(f32)
        grad_rows = field[span:]
        feed_near, feed_far = gather_group(feed_group.reshape(2, fb, -1))

        start = row * own_len - edge
        places = start + jnp.arange(span)
        inside = (places >= 0) & (places < seq)
        heads = qkv_cols // (3 * HD)
        width = -(-qkv_cols // 128) * 128
        lanes = jnp.arange(width)
        inverse = THETA ** (-(2 * (lanes % (HD // 2))).astype(f32) / HD)
        angles = places.astype(f32)[:, None] * inverse[None, :]
        turning = (lanes % (3 * HD) < 2 * HD) & (lanes < qkv_cols)
        cos_table = jnp.where(turning, jnp.cos(angles), jnp.where(lanes < qkv_cols, 1.0, 0.0))
        sine_table = jnp.where(turning, jnp.sin(angles), 0.0)
        swap = [(c * n_col + r, r * n_col + c) for r in range(n_row) for c in range(n_col)]
        documents = lax.ppermute(segments, ("row", "col"), swap)[0]
        near_documents = lax.dynamic_slice_in_dim(
            jnp.pad(documents, (edge, edge), constant_values=-1), row * own_len, span
        )
        own_documents = near_documents[edge : edge + own_len]
        own_places = places[edge : edge + own_len]
        allowed = (
            (own_documents[:, None] == near_documents[None, :])
            & (jnp.abs(own_places[:, None] - places[None, :]) <= edge)
            & inside[None, :]
        ).astype(f32)

        norm_one, inv_one = layer_norm(inputs)
        h_one = (norm_one * gain_a).astype(bf16)
        own_inputs = inputs[edge : edge + own_len]
        depth, group_cols = att_near.shape[1:]
        group_heads = heads * HD
        qkv, probs, attended, residual = pl.pallas_call(
            attend_kernel,
            grid=(n_col,),
            in_specs=[
                whole((span, width_all)), whole((own_len, width_all)),
                slot((depth, group_cols)), slot((depth, group_cols)),
                whole((span, width)), whole((span, width)), whole((own_len, span)),
            ],
            out_specs=[
                slot((span, width)), slot((heads, own_len, span)),
                slot((own_len, group_heads)), whole((own_len, width_all)),
            ],
            out_shape=[
                shape_of((n_col, span, width), bf16),
                shape_of((n_col, heads, own_len, span), f32),
                shape_of((n_col, own_len, group_heads), f32),
                shape_of((own_len, width_all), f32),
            ],
            name="attend",
        )(h_one, own_inputs, att_near, att_far, cos_table, sine_table, allowed)

        norm_two, inv_two = layer_norm(residual)
        h_two = (norm_two * gain_b).astype(bf16)
        feed_width = feed_near.shape[2]
        out_rows, grad_two, own_feed, sib_feed = pl.pallas_call(
            feed_kernel,
            grid=(n_col,),
            in_specs=[
                whole((own_len, width_all)), whole((own_len, width_all)),
                whole((own_len, width_all)),
                slot((depth, feed_width)), slot((depth, feed_width)),
            ],
            out_specs=[
                whole((own_len, width_all)), whole((own_len, width_all)),
                slot((depth, feed_width)), slot((depth, feed_width)),
            ],
            out_shape=[
                shape_of((own_len, width_all), f32),
                shape_of((own_len, width_all), f32),
                shape_of((n_col, depth, feed_width), bf16),
                shape_of((n_col, depth, feed_width), bf16),
            ],
            scratch_shapes=[pltpu.VMEM((own_len, feed_cols), bf16)],
            name="feed",
        )(h_two, grad_rows, residual, feed_near, feed_far)
        feed_done, feed_over = reduce_group(own_feed, sib_feed)
        gain_b_part = jnp.sum(grad_two * norm_two, 0)
        grad_resid = grad_rows.astype(f32) + norm_backward(grad_two, norm_two, inv_two, gain_b)

        grad_one, own_att, sib_att = pl.pallas_call(
            attend_back_kernel,
            grid=(n_col,),
            in_specs=[
                whole((own_len, width_all)), whole((span, width_all)),
                slot((depth, group_cols)), slot((depth, group_cols)),
                slot((span, width)), slot((heads, own_len, span)),
                slot((own_len, group_heads)),
                whole((span, width)), whole((span, width)),
            ],
            out_specs=[
                whole((span, width_all)),
                slot((depth, group_cols)), slot((depth, group_cols)),
            ],
            out_shape=[
                shape_of((span, width_all), f32),
                shape_of((n_col, depth, group_cols), bf16),
                shape_of((n_col, depth, group_cols), bf16),
            ],
            scratch_shapes=[pltpu.VMEM((span, width), f32)],
            name="attend_back",
        )(
            grad_resid.astype(bf16), h_one, att_near, att_far, qkv, probs, attended,
            cos_table, sine_table,
        )
        att_done, att_over = reduce_group(own_att, sib_att)
        gain_a_part = jnp.sum(grad_one * norm_one, 0)
        grad_window = norm_backward(grad_one, norm_one, inv_one, gain_a)
        grad_window = grad_window + jnp.pad(grad_resid, ((edge, edge), (0, 0)))

        def spread(value):
            parts = value.astype(bf16).T.reshape(n_row, features, -1)
            got = jnp.stack(
                [
                    parts[i] if flip == 0 else by_row(parts[i], flip)
                    for i, flip in enumerate(flips)
                ]
            )
            order = [flips.index(j) for j in range(n_row)]
            return jnp.stack(
                [
                    lax.dynamic_index_in_dim(got[jnp.array(order)], row ^ p, 0, keepdims=False)
                    for p in range(n_row)
                ]
            ).astype(f32)

        def back(value):
            return jnp.where(side == 0, value, jnp.roll(value, fb, 0))

        output = back(jnp.concatenate(list(spread(out_rows)), 1))
        windows = spread(grad_window)
        total = jnp.zeros((features, seq + 2 * edge), f32)
        for p in range(n_row):
            total = total + jnp.pad(
                windows[p],
                ((0, 0), (p * own_len, seq + 2 * edge - p * own_len - span)),
            )
        grad_tokens = back(total[:, edge : edge + seq])

        gain_parts = jnp.stack([gain_a_part, gain_b_part], 1).reshape(n_row, features, 2)
        gain_sum = gain_parts[0]
        for i, flip in enumerate(flips[1:]):
            gain_sum = gain_sum + by_row(gain_parts[i + 1], flip)
        gain_sum = lax.psum(back(gain_sum), ("dp", "col"))

        def rows_of(mine, other):
            both = jnp.concatenate([mine, other], 0).astype(f32)
            return back(both)

        att_grads = rows_of(att_done, att_over)
        feed_grads = rows_of(feed_done, feed_over)
        return (
            output,
            grad_tokens,
            gain_sum[:, 0],
            att_grads[:, :qkv_cols],
            att_grads[:, qkv_cols:].T,
            gain_sum[:, 1],
            feed_grads[:, :feed_cols].reshape(in_weight.shape),
            feed_grads[:, feed_cols:].T,
        )

    return body


def solution(mesh):
    return jax.shard_map(
        make_body(mesh),
        mesh=mesh,
        in_specs=(
            P("row", ("dp", "col")),
            P(("dp", "row"), None),
            P("row"),
            P("row", "col"),
            P("col", "row"),
            P("row"),
            P("row", None, "col"),
            P("col", "row"),
            P("row", ("dp", "col")),
        ),
        out_specs=(
            P("row", ("dp", "col")),
            P("row", ("dp", "col")),
            P("row"),
            P("row", "col"),
            P("col", "row"),
            P("row"),
            P("row", None, "col"),
            P("col", "row"),
        ),
        check_vma=False,
    )
```
